32 devices in a mesh: row: 4 (over y, core), col: 8 (over z, x).
Axes of the slice: x: 2, y: 2, z: 4, core: 2. Of those that a mesh axis runs over, the one named last changes fastest.
Arguments:
- strong_amp: float32 [512, 128, 128], P(('row', 'col')), may hold values from -3 to 3
- strong_rhs: float32 [512, 128, 128], P(('row', 'col')), may hold values from -6 to 6
- strong_left: bfloat16 [512, 128, 128], P(('row', 'col')), may hold values from -0.5 to 0.5
- strong_right: bfloat16 [512, 128, 128], P(('row', 'col')), may hold values from -0.5 to 0.5
- strong_energy: float32 [512, 128], P(('row', 'col')), may hold values from 1 to 4
- strong_intersection: bfloat16 [512, 16, 128, 128], P(('row', 'col')), may hold values from -0.375 to 0.375
- strong_nb: int32 [512, 16], P(('row', 'col')), may hold values from 0 to 39
- strong_live: int32 [512], P(('row', 'col')), may hold values from 1 to 16
- col_send: int32 [256, 2], P(('row', 'col')), may hold values from 0 to 15
- row_send: int32 [128, 2], P(('row', 'col')), may hold values from 0 to 15
- weak_amp: float32 [1024, 64, 64], P(('row', 'col')), may hold values from -3 to 3
- weak_rhs: float32 [1024, 64, 64], P(('row', 'col')), may hold values from -6 to 6
- weak_blocks: bfloat16 [1024, 64, 128], P(('row', 'col')), may hold values from -0.75 to 0.75
- weak_energy: float32 [1024, 64], P(('row', 'col')), may hold values from 1 to 4
- weak_intersection: bfloat16 [1024, 16, 64, 128], P(('row', 'col')), may hold values from -0.375 to 0.375
- weak_nb: int32 [1024, 16], P(('row', 'col')), may hold values from 0 to 39
Outputs:
- strong_next: float32 [512, 128, 128], P(('row', 'col'))
- weak_next: float32 [1024, 64, 64], P(('row', 'col'))
The draws below stay inside these ranges and needn't reach their ends.
Inputs may be any that keep to these rules, and one draw needn't show every extreme that they name: `col_send`: entries name local strong pairs of the sending device. `row_send`: entries name local strong pairs of the sending device. `strong_nb`: entries index the reading device's pool. `weak_nb`: entries index the reading device's pool. The first strong_live neighbours of a pair are in use.
All inputs are finite; a program needn't handle non-finite values.
Results may differ from the reference program's by a relative error of at most 0.0024.
Values may be sent and summed in bfloat16 or wider, within the bound.
No kernel may reach another device: no remote copies, remote signals or barrier semaphores. Data moves between devices by JAX's collectives and lax.ppermute only.
A program may use at most 128 MiB of HBM per device.

```python
import jax
import jax.numpy as jnp
from jax import lax

P_SIZE = 128
Q = 64
NB = 16
CAP = 2
UPDATES = 2
SP_DEV = 16
WP_DEV = 32
NS = 512
NW = 1024
POOL = 40
N_ROW = 4
N_COL = 8
DEVICES = 32


def with_ends(entries, own_key, least, high):
    longest = entries.shape.index(max(entries.shape))
    spots = []
    for shift in (0, 1):
        where = [jax.random.randint(jax.random.fold_in(own_key, axis), (), 0, length) for axis, length in enumerate(entries.shape)]
        where[longest] = (where[longest] + shift) % entries.shape[longest]
        spots.append(tuple(where))
    return entries.at[spots[0]].set(least).at[spots[1]].set(high)


def block_levels(own_key, shape, split, least, largest):
    gain, own = 1.0, jax.random.fold_in(own_key, 6)
    for axis_at, shards_of in split:
        steps = jnp.exp(jax.random.uniform(jax.random.fold_in(own, axis_at), (shards_of,), jnp.float32, least / len(split), largest / len(split)))
        gain = gain * jnp.repeat(steps, shape[axis_at] // shards_of).reshape([-1 if axis == axis_at else 1 for axis in range(len(shape))])
    return gain


def normal_values(own_key, dims, deviation, most, shards=(), kind=jnp.bfloat16):
    entries = jax.random.normal(own_key, dims, jnp.float32) * deviation
    if len(shards) > 0:
        entries = block_levels(own_key, dims, shards, -0.22, 0.18) * entries
    return jnp.clip(entries, min=-most, max=most).astype(kind)


def setup_inputs(seed: int = 0) -> dict:
    arg_keys = jax.random.split(jax.random.key(seed), 17)
    return {
        "strong_amp": normal_values(arg_keys[0], (NS, P_SIZE, P_SIZE), 0.5, 3.0, ((0, 32),), jnp.float32),
        "strong_rhs": normal_values(arg_keys[1], (NS, P_SIZE, P_SIZE), 1.0, 6.0, ((0, 32),), jnp.float32),
        "strong_left": normal_values(arg_keys[2], (NS, P_SIZE, P_SIZE), P_SIZE ** -0.5, 0.5, ((0, 32),)),
        "strong_right": normal_values(arg_keys[3], (NS, P_SIZE, P_SIZE), P_SIZE ** -0.5, 0.5, ((0, 32),)),
        "strong_energy": jnp.clip(1.0 + 3.0 * jax.random.uniform(arg_keys[4], (NS, P_SIZE), jnp.float32) ** block_levels(arg_keys[4], (NS, P_SIZE), ((0, 32),), -0.2, 0.2), 1.0, 4.0),
        "strong_intersection": normal_values(arg_keys[5], (NS, NB, P_SIZE, P_SIZE), (2 * P_SIZE) ** -0.5, 0.375, ((0, 32),)),
        "strong_nb": with_ends(jax.random.randint(arg_keys[6], (NS, NB), 0, POOL), jax.random.fold_in(arg_keys[6], 1), 0, POOL - 1).astype(jnp.int32),
        "strong_live": with_ends(jax.random.randint(arg_keys[7], (NS,), 1, NB + 1), jax.random.fold_in(arg_keys[7], 1), 1, NB).astype(jnp.int32),
        "col_send": with_ends(jax.random.randint(arg_keys[8], (DEVICES * N_COL, CAP), 0, SP_DEV), jax.random.fold_in(arg_keys[8], 1), 0, SP_DEV - 1).astype(jnp.int32),
        "row_send": with_ends(jax.random.randint(arg_keys[9], (DEVICES * N_ROW, CAP), 0, SP_DEV), jax.random.fold_in(arg_keys[9], 1), 0, SP_DEV - 1).astype(jnp.int32),
        "weak_amp": normal_values(arg_keys[10], (NW, Q, Q), 0.5, 3.0, ((0, 32),), jnp.float32),
        "weak_rhs": normal_values(arg_keys[11], (NW, Q, Q), 1.0, 6.0, ((0, 32),), jnp.float32),
        "weak_blocks": normal_values(arg_keys[12], (NW, Q, 2 * Q), Q ** -0.5, 0.75, ((0, 32),)),
        "weak_energy": jnp.clip(1.0 + 3.0 * jax.random.uniform(arg_keys[13], (NW, Q), jnp.float32) ** block_levels(arg_keys[13], (NW, Q), ((0, 32),), -0.2, 0.2), 1.0, 4.0),
        "weak_intersection": normal_values(arg_keys[14], (NW, NB, Q, P_SIZE), (2 * P_SIZE) ** -0.5, 0.375, ((0, 32),)),
        "weak_nb": with_ends(jax.random.randint(arg_keys[15], (NW, NB), 0, POOL), jax.random.fold_in(arg_keys[15], 1), 0, POOL - 1).astype(jnp.int32),
    }


def gather_pool(tiles, col_lists, row_lists, row_index, col_index):
    col_ids = jnp.arange(N_COL, dtype=jnp.int32)[:, None]
    row_ids = jnp.arange(N_ROW, dtype=jnp.int32)[:, None]
    own_row = tiles[row_index]
    col_pool = own_row[col_ids, col_lists[row_index, :, col_index, :]]
    own_col = tiles[:, col_index]
    row_pool = own_col[row_ids, row_lists[:, col_index, row_index, :]]
    local = own_row[col_index]
    return jnp.concatenate([local, col_pool.reshape(-1, P_SIZE, P_SIZE), row_pool.reshape(-1, P_SIZE, P_SIZE)], axis=0)


def sandwich(intersection, gathered, live_mask):
    half_way = jnp.einsum('snab,snbc->snac', intersection.astype(jnp.float32), gathered.astype(jnp.float32))
    half_way = half_way.astype(jnp.bfloat16).astype(jnp.float32) * live_mask
    return jnp.einsum('snac,sndc->sad', half_way, intersection.astype(jnp.float32))


def advance(amplitude, rhs, left, right, energy, coupling):
    tiles_now = amplitude.astype(jnp.bfloat16).astype(jnp.float32)
    inter = jnp.einsum('sab,sbc->sac', left.astype(jnp.float32), tiles_now)
    inter = inter + jnp.einsum('sab,sbc->sac', tiles_now, right.astype(jnp.float32))
    residual = rhs + inter + coupling
    return amplitude - residual / (energy[:, :, None] + energy[:, None, :])


def reference(strong_amp, strong_rhs, strong_left, strong_right, strong_energy, strong_intersection, strong_nb, strong_live, col_send, row_send, weak_amp, weak_rhs, weak_blocks, weak_energy, weak_intersection, weak_nb):
    count = N_ROW * N_COL
    col_lists = col_send.reshape(N_ROW, N_COL, N_COL, CAP)
    row_lists = row_send.reshape(N_ROW, N_COL, N_ROW, CAP)
    fixed_items = (
        strong_rhs.reshape(count, SP_DEV, P_SIZE, P_SIZE),
        strong_left.reshape(count, SP_DEV, P_SIZE, P_SIZE),
        strong_right.reshape(count, SP_DEV, P_SIZE, P_SIZE),
        strong_energy.reshape(count, SP_DEV, P_SIZE),
        strong_intersection.reshape(count, SP_DEV, NB, P_SIZE, P_SIZE),
        strong_nb.reshape(count, SP_DEV, NB),
        strong_live.reshape(count, SP_DEV),
        weak_rhs.reshape(count, WP_DEV, Q, Q),
        weak_blocks.reshape(count, WP_DEV, Q, 2 * Q),
        weak_energy.reshape(count, WP_DEV, Q),
        weak_intersection.reshape(count, WP_DEV, NB, Q, P_SIZE),
        weak_nb.reshape(count, WP_DEV, NB),
    )
    indices = jnp.arange(count, dtype=jnp.int32)
    for update_step in range(UPDATES):
        tiles = strong_amp.astype(jnp.bfloat16).reshape(N_ROW, N_COL, SP_DEV, P_SIZE, P_SIZE)

        def per_device(items):
            index, amplitude, weak_now, rhs, left, right, energy, intersection, neighbours, live, wrhs, wblocks, wenergy, woverlap, wneighbours = items
            row_index = index // N_COL
            col_index = index % N_COL
            tile_pool = gather_pool(tiles, col_lists, row_lists, row_index, col_index)
            live_mask = (jnp.arange(NB, dtype=jnp.int32)[None, :] < live[:, None]).astype(jnp.float32)[:, :, None, None]
            strong = advance(amplitude, rhs, left, right, energy, sandwich(intersection, tile_pool[neighbours], live_mask))
            ones = jnp.ones((WP_DEV, NB, 1, 1), jnp.float32)
            weak_coupling = sandwich(woverlap, tile_pool[wneighbours], ones)
            weak = advance(weak_now, wrhs, wblocks[:, :, :Q], wblocks[:, :, Q:], wenergy, weak_coupling)
            return strong, weak

        strong_blocks, weak_blocks_new = lax.map(per_device, (indices, strong_amp.reshape(count, SP_DEV, P_SIZE, P_SIZE), weak_amp.reshape(count, WP_DEV, Q, Q)) + fixed_items)
        strong_amp = strong_blocks.reshape(count * SP_DEV, P_SIZE, P_SIZE)
        weak_amp = weak_blocks_new.reshape(count * WP_DEV, Q, Q)
    return strong_amp, weak_amp
```

```python
import functools

import jax
import jax.numpy as jnp
from jax import lax
from jax.experimental import pallas as pl
from jax.experimental.pallas import tpu as pltpu
from jax.sharding import PartitionSpec as P

UPDATES = 2
F32 = jnp.float32
BF16 = jnp.bfloat16
VMEM = pltpu.VMEM
MIB = 1 << 20


def vmem():
    return pl.BlockSpec(memory_space=pltpu.VMEM)


def smem():
    return pl.BlockSpec(memory_space=pltpu.SMEM)


def call(body, outs, in_specs, flops, nbytes, scratch=(), limit=8 * MIB):
    return pl.pallas_call(
        body,
        out_shape=[jax.ShapeDtypeStruct(s, d) for s, d in outs],
        in_specs=in_specs,
        out_specs=[vmem() for _ in outs],
        scratch_shapes=list(scratch),
        cost_estimate=pl.CostEstimate(
            flops=int(flops), bytes_accessed=int(nbytes), transcendentals=0
        ),
        compiler_params=pltpu.CompilerParams(vmem_limit_bytes=limit),
    )


def dot(a, b):
    return jnp.dot(a, b, preferred_element_type=F32)


def dot_t(a, b):
    return lax.dot_general(a, b, (((1,), (1,)), ((), ())), preferred_element_type=F32)


def partner(i, k, n):
    return i ^ k if n & (n - 1) == 0 else lax.rem(i + k, n)


def origin(i, k, n):
    return i ^ k if n & (n - 1) == 0 else lax.rem(i + n - k, n)


def perm(k, n):
    if n & (n - 1) == 0:
        return [(s, s ^ k) for s in range(n)]
    return [(s, (s + k) % n) for s in range(n)]


def fill_sends(me, tiles, col_send, row_send, col_out, row_out):
    for out, lists, i in ((col_out, col_send, me[1]), (row_out, row_send, me[0])):
        n = len(out) + 1
        for k in range(1, n):
            d = partner(i, k, n)
            for s in range(out[0].shape[0]):
                out[k - 1][s] = tiles[lists[d, s]]


def prep_kernel(nc, nr, me, amp, col_send, row_send, tiles, *sends):
    def body(i, c):
        tiles[i] = amp[i].astype(BF16)
        return c

    lax.fori_loop(0, amp.shape[0], body, 0)
    fill_sends(me, tiles, col_send, row_send, sends[: nc - 1], sends[nc - 1 :])


def weak_inter(blocks, t):
    q = t.shape[0]
    return dot(blocks[:, :q], t) + dot(t, blocks[:, q:])


def load_kernel(
    tiles, s_rhs, s_left, s_right, s_energy, w_amp, w_rhs, w_blocks, w_energy, s_int, w_int,
    s_all, w_all, s_base, w_base, s_inv, w_inv, sem,
):
    copies = [
        pltpu.make_async_copy(s_int, s_all, sem.at[0]),
        pltpu.make_async_copy(w_int, w_all, sem.at[1]),
    ]
    for c in copies:
        c.start()

    def inverse(e):
        n = e.shape[1]
        rows = jnp.broadcast_to(e, (n, n))
        return 1.0 / (rows.T + rows)

    def strong(p, c):
        t = tiles[p]
        s_base[p] = s_rhs[p] + dot(s_left[p], t) + dot(t, s_right[p])
        s_inv[p] = inverse(s_energy[pl.ds(p, 1), :])
        return c

    def weak(w, c):
        t = w_amp[w].astype(BF16)
        w_base[w] = w_rhs[w] + weak_inter(w_blocks[w], t)
        w_inv[w] = inverse(w_energy[pl.ds(w, 1), :])
        return c

    lax.fori_loop(0, tiles.shape[0], strong, 0)
    lax.fori_loop(0, w_amp.shape[0], weak, 0)
    for c in copies:
        c.wait()


def build_pool(nc, nr, me, pool, tiles, col_send, row_send, recv):
    own = tiles.shape[0]
    cap = recv[0].shape[0]

    def body(i, c):
        pool[i] = tiles[i]
        return c

    lax.fori_loop(0, own, body, 0)
    at = own
    for got, lists, i, n in (
        (recv[: nc - 1], col_send, me[1], nc),
        (recv[nc - 1 :], row_send, me[0], nr),
    ):
        for s in range(cap):
            pool[at + i * cap + s] = tiles[lists[i, s]]
        for k in range(1, n):
            o = origin(i, k, n)
            for s in range(cap):
                pool[at + o * cap + s] = got[k - 1][s]
        at += n * cap


def strong_coupling(p, pool, nb, live, inter):
    count = inter.shape[1]
    mids = []
    for n in range(count):
        m = dot(inter[p, n], pool[nb[p, n]]).astype(BF16)
        mids.append(jnp.where(n < live[p], m, jnp.zeros_like(m)))
    return dot_t(
        jnp.concatenate(mids, axis=1),
        jnp.concatenate([inter[p, n] for n in range(count)], axis=1),
    )


def weak_coupling(w, pool, nb, inter):
    count, q = inter.shape[1:3]
    mids = []
    for n in range(0, count, 2):
        both = jnp.concatenate([inter[w, n], inter[w, n + 1]], axis=0)
        xs = jnp.concatenate([pool[nb[w, n]], pool[nb[w, n + 1]]], axis=1)
        m = dot(both, xs)
        width = m.shape[1] // 2
        mids.append(m[:q, :width].astype(BF16))
        mids.append(m[q:, width:].astype(BF16))
    return dot_t(
        jnp.concatenate(mids, axis=1),
        jnp.concatenate([inter[w, n] for n in range(count)], axis=1),
    )


def pairs_loop(n, f, unroll=2):
    def body(i, c):
        for u in range(unroll):
            f(i * unroll + u)
        return c

    lax.fori_loop(0, n // unroll, body, 0)


def strong_kernel(nc, nr, me, nb, live, col_send, row_send, tiles, s_all, s_base, s_inv, amp, *rest):
    m = nc + nr - 2
    recv, (pool, amp_out, tiles_out), sends = rest[:m], rest[m : m + 3], rest[m + 3 :]
    build_pool(nc, nr, me, pool, tiles, col_send, row_send, recv)

    def one(p):
        c = strong_coupling(p, pool, nb, live, s_all)
        new = amp[p] - (s_base[p] + c) * s_inv[p]
        amp_out[p] = new
        tiles_out[p] = new.astype(BF16)

    pairs_loop(nb.shape[0], one)
    fill_sends(me, tiles_out, col_send, row_send, sends[: nc - 1], sends[nc - 1 :])


def weak_kernel(
    nb, pool, w_all, w_base, w_inv, w_amp, w_rhs, w_blocks, tiles, s_rhs, s_left, s_right,
    w_out, w_base_out, s_base_out,
):
    def one(w):
        c = weak_coupling(w, pool, nb, w_all)
        new = w_amp[w] - (w_base[w] + c) * w_inv[w]
        w_out[w] = new
        w_base_out[w] = w_rhs[w] + weak_inter(w_blocks[w], new.astype(BF16))

    pairs_loop(nb.shape[0], one)

    def strong(p):
        t = tiles[p]
        s_base_out[p] = s_rhs[p] + dot(s_left[p], t) + dot(t, s_right[p])

    pairs_loop(tiles.shape[0], strong)


def last_kernel(
    nc, nr, me, s_nb, live, w_nb, col_send, row_send, tiles, s_all, w_all, s_base, s_inv, s_amp, w_base, w_inv, w_amp, *rest
):
    m = nc + nr - 2
    recv, (s_out, w_out, pool) = rest[:m], rest[m:]
    build_pool(nc, nr, me, pool, tiles, col_send, row_send, recv)

    def strong(p):
        c = strong_coupling(p, pool, s_nb, live, s_all)
        s_out[p] = s_amp[p] - (s_base[p] + c) * s_inv[p]

    def weak(w):
        c = weak_coupling(w, pool, w_nb, w_all)
        w_out[w] = w_amp[w] - (w_base[w] + c) * w_inv[w]

    pairs_loop(s_nb.shape[0], strong)
    pairs_loop(w_nb.shape[0], weak)


def on_device(
    nr, nc, strong_amp, strong_rhs, strong_left, strong_right, strong_energy, strong_intersection,
    strong_nb, strong_live, col_send, row_send, weak_amp, weak_rhs, weak_blocks, weak_energy,
    weak_intersection, weak_nb,
):
    sp, width = strong_amp.shape[:2]
    wp, q = weak_amp.shape[:2]
    nbs = strong_nb.shape[1]
    cap = col_send.shape[1]
    n_pool = sp + cap * (nc + nr)
    me = jnp.stack([lax.axis_index("row"), lax.axis_index("col")]).astype(jnp.int32)
    s_shape = (sp, width, width)
    w_shape = (wp, q, q)
    send_shapes = [((cap, width, width), BF16)] * (nc + nr - 2)
    s_flops = 4 * sp * nbs * width**3
    w_flops = 2 * wp * nbs * (q * width * width + q * q * width)
    a_flops = 4 * sp * width**3

    def exchange(sends):
        out = []
        for k in range(1, nc):
            out.append(lax.ppermute(sends[k - 1], "col", perm(k, nc)))
        for k in range(1, nr):
            out.append(lax.ppermute(sends[nc - 2 + k], "row", perm(k, nr)))
        return out

    tiles, *sends = call(
        functools.partial(prep_kernel, nc, nr),
        [(s_shape, BF16)] + send_shapes,
        [smem(), vmem(), smem(), smem()],
        0, strong_amp.size * 4,
    )(me, strong_amp, col_send, row_send)
    recv = exchange(sends)
    s_all, w_all, s_base, w_base, s_inv, w_inv = call(
        load_kernel,
        [
            (strong_intersection.shape, BF16), (weak_intersection.shape, BF16),
            (s_shape, F32), (w_shape, F32), (s_shape, F32), (w_shape, F32),
        ],
        [vmem()] * 9 + [pl.BlockSpec(memory_space=pl.ANY)] * 2,
        a_flops, (strong_intersection.size + weak_intersection.size) * 2,
        [pltpu.SemaphoreType.DMA((2,))],
    )(
        tiles, strong_rhs, strong_left, strong_right, strong_energy, weak_amp, weak_rhs,
        weak_blocks, weak_energy, strong_intersection, weak_intersection,
    )
    pool, amp1, tiles1, *sends1 = call(
        functools.partial(strong_kernel, nc, nr),
        [((n_pool, width, width), BF16), (s_shape, F32), (s_shape, BF16)] + send_shapes,
        [smem()] * 5 + [vmem()] * (5 + nc + nr - 2),
        s_flops, strong_amp.size * 8,
    )(me, strong_nb, strong_live, col_send, row_send, tiles, s_all, s_base, s_inv, strong_amp, *recv)
    recv1 = exchange(sends1)
    w_amp1, w_base1, s_base1 = call(
        weak_kernel,
        [(w_shape, F32), (w_shape, F32), (s_shape, F32)],
        [smem()] + [vmem()] * 11,
        w_flops + a_flops, weak_amp.size * 8,
    )(
        weak_nb, pool, w_all, w_base, w_inv, weak_amp, weak_rhs, weak_blocks, tiles1,
        strong_rhs, strong_left, strong_right,
    )
    s_out, w_out = call(
        functools.partial(last_kernel, nc, nr),
        [(s_shape, F32), (w_shape, F32)],
        [smem()] * 6 + [vmem()] * (9 + nc + nr - 2),
        s_flops + w_flops, strong_amp.size * 8,
        [pltpu.VMEM((n_pool, width, width), BF16)],
    )(
        me, strong_nb, strong_live, weak_nb, col_send, row_send, tiles1, s_all, w_all, s_base1,
        s_inv, amp1, w_base1, w_inv, w_amp1, *recv1,
    )
    return s_out, w_out


def solution(mesh):
    nr, nc = mesh.shape["row"], mesh.shape["col"]
    whole = ("row", "col")
    ranks = (3, 3, 3, 3, 2, 4, 2, 1, 2, 2, 3, 3, 3, 2, 4, 2)
    in_specs = tuple(P(whole, *(None,) * (r - 1)) for r in ranks)
    out_specs = (P(whole, None, None), P(whole, None, None))
    return jax.shard_map(
        functools.partial(on_device, nr, nc),
        mesh=mesh, in_specs=in_specs, out_specs=out_specs, check_vma=False,
    )
```

```python
import functools

import jax
import jax.numpy as jnp
from jax import lax
from jax.experimental import pallas as pl
from jax.experimental.pallas import tpu as pltpu
from jax.sharding import PartitionSpec as P

F32 = jnp.float32
BF16 = jnp.bfloat16
MIB = 1 << 20
GROUP = 4
STRONG_ITEMS = 4
WEAK_ITEMS = 8
SHIFT = 8


VM = pl.BlockSpec(memory_space=pltpu.VMEM)
SM = pl.BlockSpec(memory_space=pltpu.SMEM)
HB = pl.BlockSpec(memory_space=pltpu.HBM)
ANY = pl.BlockSpec(memory_space=pl.ANY)


def call(body, outs, in_specs, flops, nbytes, scratch):
    return pl.pallas_call(
        body,
        out_shape=[jax.ShapeDtypeStruct(s, d) for s, d in outs],
        in_specs=in_specs,
        out_specs=[HB for _ in outs],
        scratch_shapes=list(scratch),
        cost_estimate=pl.CostEstimate(
            flops=int(flops), bytes_accessed=int(nbytes), transcendentals=0
        ),
        compiler_params=pltpu.CompilerParams(vmem_limit_bytes=60 * 1024 * 1024),
    )


class Copies:
    def __init__(self, sems):
        self.sems, self.used, self.named = sems, 0, {}

    def start(self, name, src, dst):
        copy = pltpu.make_async_copy(src, dst, self.sems.at[self.used])
        self.used += 1
        self.named.setdefault(name, []).append(copy)
        copy.start()

    def wait(self, *names):
        for name in names:
            for copy in self.named.pop(name):
                copy.wait()


def dot(a, b):
    return jnp.dot(a, b, preferred_element_type=F32)


def dot_t(a, b):
    return lax.dot_general(a, b, (((1,), (1,)), ((), ())), preferred_element_type=F32)


def partner(i, k, n):
    return i ^ k if n & (n - 1) == 0 else lax.rem(i + k, n)


def origin(i, k, n):
    return i ^ k if n & (n - 1) == 0 else lax.rem(i + n - k, n)


def perm(k, n):
    if n & (n - 1) == 0:
        return [(s, s ^ k) for s in range(n)]
    return [(s, (s + k) % n) for s in range(n)]


def each(n, f, unroll=1):
    if n % unroll:
        unroll = 1

    def body(i, c):
        for u in range(unroll):
            f(i * unroll + u)
        return c

    lax.fori_loop(0, n // unroll, body, 0)


def start_sends(copies, me, tiles, col_send, row_send, col_out, row_out):
    cap = col_out.shape[1]
    for d in range(col_out.shape[0]):
        for s in range(cap):
            copies.start("sent", tiles.at[col_send[d, s]], col_out.at[d, s])
    n = len(row_out) + 1
    for k in range(1, n):
        d = partner(me[0], k, n)
        for s in range(cap):
            copies.start("sent", tiles.at[row_send[d, s]], row_out[k - 1].at[s])


def prep_kernel(me, col_send_h, row_send_h, amp_h, tiles_out, col_out, *rest):
    *row_out, amp, tiles, col_send, row_send, sems = rest
    copies = Copies(sems)
    parts = 4
    step = amp.shape[0] // parts
    copies.start("lists", col_send_h, col_send)
    copies.start("lists", row_send_h, row_send)
    for i in range(parts):
        at = pl.ds(i * step, step)
        copies.start(i, amp_h.at[at], amp.at[at])
    for i in range(parts):
        copies.wait(i)
        for j in range(step):
            tiles[i * step + j] = amp[i * step + j].astype(BF16)
    copies.wait("lists")
    start_sends(copies, me, tiles, col_send, row_send, col_out, row_out)
    copies.start("sent", tiles, tiles_out)
    copies.wait("sent")


def weak_inter(blocks, t):
    q = t.shape[0]
    return dot(blocks[:, :q], t) + dot(t, blocks[:, q:])


def strong_inter(left, right, t):
    return dot(left, t) + dot(t, right)


def inverse(e):
    n = e.shape[1]
    rows = jnp.broadcast_to(e, (n, n))
    return 1.0 / (rows.T + rows)


def start_near(copies, me, tiles, col_send, row_send, pool, nc):
    own = tiles.shape[0]
    cap = col_send.shape[1]
    copies.start("near", tiles, pool.at[pl.ds(0, own)])
    for s in range(cap):
        copies.start("near", tiles.at[col_send[me[1], s]], pool.at[own + me[1] * cap + s])
        copies.start(
            "near", tiles.at[row_send[me[0], s]], pool.at[own + (nc + me[0]) * cap + s]
        )


def start_pool(copies, me, tiles, row_send, pool, got, row_got):
    own = tiles.shape[0]
    nc, cap = got.shape[:2]
    copies.start("near", tiles, pool.at[pl.ds(0, own)])
    for c in range(nc):
        copies.start("near", got.at[c], pool.at[pl.ds(own + c * cap, cap)])
    at = own + nc * cap
    n = len(row_got) + 1
    for s in range(cap):
        copies.start("near", tiles.at[row_send[me[0], s]], pool.at[at + me[0] * cap + s])
    for k in range(1, n):
        o = origin(me[0], k, n)
        copies.start("near", row_got[k - 1], pool.at[pl.ds(at + o * cap, cap)])


class Rows:
    def __init__(self, src, dst, sems):
        self.src, self.dst, self.sems = src, dst, sems
        self.n = dst.shape[0]

    def copy(self, i):
        return pltpu.make_async_copy(self.src.at[i], self.dst.at[i], self.sems.at[i])

    def start(self):
        for i in range(self.n):
            self.copy(i).start()

    def wait(self, ready, upto):
        def one(i, c):
            self.copy(i).wait()
            return c

        lax.fori_loop(ready, upto, one, 0)
        return jnp.maximum(ready, upto)


def make_list(items, n, near, total, phase, step):
    most = GROUP

    def one(p, at):
        full = near[p] >> 2
        if phase == 0:
            first, count = 0, full
        else:
            first, count = full, total(p) - full
        for j in range(most):
            items[at + j] = p * most + first + j
        return at + count

    count = lax.fori_loop(0, n, one, 0)
    for j in range(step):
        items[count + j] = n * most
    return (count + step - 1) // step


def run_items(items, steps, step, pool, order, inter, rows, acc, live):
    n = inter.shape[0]

    def body(i, ready):
        last = jnp.minimum(items[i * step + step - 1] >> 2, n - 1)
        ready = rows.wait(ready, last + 1)
        for u in range(step):
            item = items[i * step + u]
            at = item >> 2
            p = jnp.minimum(at, n - 1)
            j = (item & 3) * GROUP
            mids, weights = [], []
            for g in range(GROUP):
                e = order[p, j + g]
                w = inter[p, e >> SHIFT]
                m = dot(w, pool[e & ((1 << SHIFT) - 1)]).astype(BF16)
                if live is not None:
                    m = jnp.where(j + g < live[p], m, jnp.zeros_like(m))
                mids.append(m)
                weights.append(w)
            acc[at] += dot_t(jnp.concatenate(mids, axis=1), jnp.concatenate(weights, axis=1))
        return ready

    ready = lax.fori_loop(0, steps, body, jnp.int32(0))
    rows.wait(ready, n)


def run_strong(phase, items, pool, order, near, live, inter, rows, acc):
    n = inter.shape[0]
    steps = make_list(items, n, near, lambda p: (live[p] + 3) >> 2, phase, STRONG_ITEMS)
    run_items(items, steps, STRONG_ITEMS, pool, order, inter, rows, acc, live)


def run_weak(phase, items, pool, order, near, inter, rows, acc):
    n, count = inter.shape[:2]
    steps = make_list(items, n, near, lambda p: count >> 2, phase, WEAK_ITEMS)
    run_items(items, steps, WEAK_ITEMS, pool, order, inter, rows, acc, None)


def first_kernel(
    nc, me, s_order, s_near, live, w_order, w_near, col_send, row_send,
    tiles_h, s_rhs_h, s_left_h, s_right_h, s_energy_h, w_amp_h, w_rhs_h, w_blocks_h, w_energy_h,
    s_int_h, w_int_h,
    s_acc_out, w_acc_out, s_inv_out, w_inv_out,
    pool, s_rhs, s_left, s_right, s_energy, w_amp, w_rhs, w_blocks, w_energy, s_all, w_all,
    s_acc, w_acc, s_inv, w_inv, s_items, w_items, sems, s_sems, w_sems,
):
    copies = Copies(sems)
    start_near(copies, me, tiles_h, col_send, row_send, pool, nc)
    for src, dst in ((s_left_h, s_left), (s_right_h, s_right), (s_rhs_h, s_rhs), (s_energy_h, s_energy)):
        copies.start("s", src, dst)
    for src, dst in ((w_amp_h, w_amp), (w_blocks_h, w_blocks), (w_rhs_h, w_rhs), (w_energy_h, w_energy)):
        copies.start("w", src, dst)
    s_rows, w_rows = Rows(s_int_h, s_all, s_sems), Rows(w_int_h, w_all, w_sems)
    s_rows.start()
    w_rows.start()
    copies.wait("near", "s")

    def strong(p):
        s_acc[p] = s_rhs[p] + strong_inter(s_left[p], s_right[p], pool[p])
        s_inv[p] = inverse(s_energy[pl.ds(p, 1), :])

    each(s_rhs.shape[0], strong, 2)
    copies.wait("w")

    def weak(w):
        w_acc[w] = w_rhs[w] + weak_inter(w_blocks[w], w_amp[w].astype(BF16))
        w_inv[w] = inverse(w_energy[pl.ds(w, 1), :])

    each(w_amp.shape[0], weak, 2)
    copies.start("out", s_inv, s_inv_out)
    copies.start("out", w_inv, w_inv_out)
    run_strong(0, s_items, pool, s_order, s_near, live, s_all, s_rows, s_acc)
    copies.start("out", s_acc.at[pl.ds(0, s_inv.shape[0])], s_acc_out)
    run_weak(0, w_items, pool, w_order, w_near, w_all, w_rows, w_acc)
    copies.start("out", w_acc.at[pl.ds(0, w_inv.shape[0])], w_acc_out)
    copies.wait("out")


def strong_kernel(
    me, s_order, s_near, live, col_send, row_send, tiles_h, got, s_int_h, s_acc_h, s_inv_h, amp_h,
    *rest,
):
    n_row = (len(rest) - 12) // 2
    row_got, (amp_out, tiles_out, col_out), row_out = (
        rest[:n_row], rest[n_row : n_row + 3], rest[n_row + 3 : 2 * n_row + 3]
    )
    pool, s_all, s_acc, s_inv, amp, tiles, s_items, sems, s_sems = rest[2 * n_row + 3 :]
    n = amp.shape[0]
    copies = Copies(sems)
    start_pool(copies, me, tiles_h, row_send, pool, got, row_got)
    copies.start("acc", s_acc_h, s_acc.at[pl.ds(0, n)])
    rows = Rows(s_int_h, s_all, s_sems)
    rows.start()
    copies.start("end", amp_h, amp)
    copies.start("end", s_inv_h, s_inv)
    copies.wait("near", "acc")
    run_strong(1, s_items, pool, s_order, s_near, live, s_all, rows, s_acc)
    copies.wait("end")

    def finish(p):
        new = amp[p] - s_acc[p] * s_inv[p]
        amp[p] = new
        tiles[p] = new.astype(BF16)

    each(n, finish, 2)
    start_sends(copies, me, tiles, col_send, row_send, col_out, row_out)
    copies.start("sent", tiles, tiles_out)
    copies.start("sent", amp, amp_out)
    copies.wait("sent")


def middle_kernel(
    nc, me, s_order, s_near, live, w_order, w_near, col_send, row_send,
    tiles_h, got, tiles1_h, w_acc_h, w_inv_h, w_amp_h, w_rhs_h, w_blocks_h, s_rhs_h, s_left_h,
    s_right_h, s_int_h, w_int_h, *rest,
):
    n_row = len(rest) - 20
    row_got, (w_out, s_acc_out, w_acc_out) = rest[:n_row], rest[n_row : n_row + 3]
    (
        pool, pool1, w_acc, w_inv, w_amp, w_rhs, w_blocks, s_rhs, s_left, s_right, s_all, w_all,
        s_acc, s_items, w_items, sems, s_sems,
    ) = rest[n_row + 3 :]
    wp = w_amp.shape[0]
    w_sems = s_sems.at[1]
    copies = Copies(sems)
    start_pool(copies, me, tiles_h, row_send, pool, got, row_got)
    copies.start("acc", w_acc_h, w_acc.at[pl.ds(0, wp)])
    w_rows = Rows(w_int_h, w_all, w_sems)
    w_rows.start()
    for src, dst in ((w_inv_h, w_inv), (w_amp_h, w_amp), (w_rhs_h, w_rhs), (w_blocks_h, w_blocks)):
        copies.start("w", src, dst)
    copies.wait("near", "acc")
    start_near(copies, me, tiles1_h, col_send, row_send, pool1, nc)
    for src, dst in ((s_left_h, s_left), (s_right_h, s_right), (s_rhs_h, s_rhs)):
        copies.start("s", src, dst)
    s_rows = Rows(s_int_h, s_all, s_sems.at[0])
    s_rows.start()
    run_weak(1, w_items, pool, w_order, w_near, w_all, w_rows, w_acc)
    copies.wait("w")

    def weak(w):
        new = w_amp[w] - w_acc[w] * w_inv[w]
        w_amp[w] = new
        w_acc[w] = w_rhs[w] + weak_inter(w_blocks[w], new.astype(BF16))

    each(wp, weak, 4)
    copies.start("out", w_amp, w_out)
    copies.wait("near", "s")

    def strong(p):
        s_acc[p] = s_rhs[p] + strong_inter(s_left[p], s_right[p], pool1[p])

    each(s_rhs.shape[0], strong, 2)
    run_strong(0, s_items, pool1, s_order, s_near, live, s_all, s_rows, s_acc)
    copies.start("out", s_acc.at[pl.ds(0, s_rhs.shape[0])], s_acc_out)
    run_weak(0, w_items, pool1, w_order, w_near, w_all, NoRows(), w_acc)
    copies.start("out", w_acc.at[pl.ds(0, wp)], w_acc_out)
    copies.wait("out")


class NoRows:
    def wait(self, ready, upto):
        return ready


def last_kernel(
    me, s_order, s_near, live, w_order, w_near, row_send, tiles_h, got, s_int_h, w_int_h, s_acc_h,
    w_acc_h, s_inv_h, w_inv_h, s_amp_h, w_amp_h, *rest,
):
    n_row = len(rest) - 16
    row_got, (s_out, w_out) = rest[:n_row], rest[n_row : n_row + 2]
    (
        pool, s_all, w_all, s_acc, w_acc, s_inv, w_inv, s_amp, w_amp, s_items, w_items, sems,
        s_sems, w_sems,
    ) = rest[n_row + 2 :]
    n, wp = s_amp.shape[0], w_amp.shape[0]
    copies = Copies(sems)
    start_pool(copies, me, tiles_h, row_send, pool, got, row_got)
    copies.start("s", s_acc_h, s_acc.at[pl.ds(0, n)])
    s_rows, w_rows = Rows(s_int_h, s_all, s_sems), Rows(w_int_h, w_all, w_sems)
    s_rows.start()
    copies.start("s_end", s_amp_h, s_amp)
    copies.start("s_end", s_inv_h, s_inv)
    copies.start("w", w_acc_h, w_acc.at[pl.ds(0, wp)])
    w_rows.start()
    copies.start("w_end", w_amp_h, w_amp)
    copies.start("w_end", w_inv_h, w_inv)
    copies.wait("near", "s")
    run_strong(1, s_items, pool, s_order, s_near, live, s_all, s_rows, s_acc)
    copies.wait("s_end")

    def strong(p):
        s_amp[p] = s_amp[p] - s_acc[p] * s_inv[p]

    each(n, strong, 2)
    copies.start("out", s_amp, s_out)
    copies.wait("w")
    run_weak(1, w_items, pool, w_order, w_near, w_all, w_rows, w_acc)
    copies.wait("w_end")

    def weak(w):
        w_amp[w] = w_amp[w] - w_acc[w] * w_inv[w]

    each(wp, weak, 4)
    copies.start("out", w_amp, w_out)
    copies.wait("out")


def ordered(nb, far, live):
    count = nb.shape[1]
    place = jnp.arange(count, dtype=jnp.int32)
    used = place[None, :] < live[:, None]
    key = jnp.where(used, jnp.where(far, count, 0), 2 * count) + place[None, :]
    at = jnp.sum((key[:, None, :] < key[:, :, None]).astype(jnp.int32), axis=2)
    packed = (place[None, :] << SHIFT) + nb
    order = jnp.sum(jnp.where(at[:, :, None] == place[None, None, :], packed[:, :, None], 0), axis=1)
    near = jnp.sum((used & ~far).astype(jnp.int32), axis=1)
    return order, near


def on_device(
    nr, nc, strong_amp, strong_rhs, strong_left, strong_right, strong_energy, strong_intersection,
    strong_nb, strong_live, col_send, row_send, weak_amp, weak_rhs, weak_blocks, weak_energy,
    weak_intersection, weak_nb,
):
    sp, width = strong_amp.shape[:2]
    wp, q = weak_amp.shape[:2]
    count = strong_nb.shape[1]
    cap = col_send.shape[1]
    row, col = lax.axis_index("row"), lax.axis_index("col")
    me = jnp.stack([row, col]).astype(jnp.int32)
    s_shape, w_shape = (sp, width, width), (wp, q, q)
    s_f32, w_f32 = pltpu.VMEM(s_shape, F32), pltpu.VMEM(w_shape, F32)
    s_bf16, blocks = pltpu.VMEM(s_shape, BF16), pltpu.VMEM(weak_blocks.shape, BF16)
    s_sums = pltpu.VMEM((sp + 1, width, width), F32)
    w_sums = pltpu.VMEM((wp + 1, q, q), F32)
    s_all = pltpu.VMEM(strong_intersection.shape, BF16)
    w_all = pltpu.VMEM(weak_intersection.shape, BF16)
    pool = pltpu.VMEM((sp + cap * (nc + nr), width, width), BF16)
    row_shapes = [((cap, width, width), BF16)] * (nr - 1)
    col_shape = ((nc, cap, width, width), BF16)
    s_flops = 4 * sp * count * width**3
    w_flops = 2 * wp * count * (q * width * width + q * q * width)
    a_flops = 4 * sp * width**3
    s_bytes, w_bytes = strong_intersection.size * 2, weak_intersection.size * 2
    s_items = pltpu.SMEM((sp * count // GROUP + GROUP + STRONG_ITEMS,), jnp.int32)
    w_items = pltpu.SMEM((wp * count // GROUP + GROUP + WEAK_ITEMS,), jnp.int32)
    sem = pltpu.SemaphoreType.DMA
    pool_sems = nc + nr + cap + 4 * cap
    sent_sems = cap * (nc + nr) + 2

    def far(nb):
        own = sp + col * cap
        own_row = sp + (nc + row) * cap
        mine = (nb < sp) | ((nb >= own) & (nb < own + cap)) | ((nb >= own_row) & (nb < own_row + cap))
        return ~mine

    s_order, s_near = ordered(strong_nb, far(strong_nb), strong_live)
    w_order, w_near = ordered(weak_nb, far(weak_nb), jnp.full((wp,), count, jnp.int32))

    def exchange(col_out, row_out):
        got = lax.all_to_all(col_out, "col", split_axis=0, concat_axis=0, tiled=True)
        return got, [lax.ppermute(x, "row", perm(k + 1, nr)) for k, x in enumerate(row_out)]

    tiles, col_out, *row_out = call(
        prep_kernel,
        [(s_shape, BF16), col_shape] + row_shapes,
        [SM, HB, HB, HB],
        0, strong_amp.size * 8,
        [
            s_f32, s_bf16, pltpu.SMEM(col_send.shape, jnp.int32),
            pltpu.SMEM(row_send.shape, jnp.int32), sem((sent_sems + 6,)),
        ],
    )(me, col_send, row_send, strong_amp)
    got, row_got = exchange(col_out, row_out)
    s_acc, w_acc, s_inv, w_inv = call(
        functools.partial(first_kernel, nc),
        [(s_shape, F32), (w_shape, F32)] * 2,
        [SM] * 8 + [HB] * 11,
        a_flops + (s_flops + w_flops) // 2, s_bytes + w_bytes,
        [
            pool, s_f32, s_bf16, s_bf16, pltpu.VMEM(strong_energy.shape, F32), w_f32, w_f32,
            blocks, pltpu.VMEM(weak_energy.shape, F32), s_all, w_all, s_sums, w_sums, s_f32, w_f32,
            s_items, w_items, sem((pool_sems + 12,)), sem((sp,)), sem((wp,)),
        ],
    )(
        me, s_order, s_near, strong_live, w_order, w_near, col_send, row_send,
        tiles, strong_rhs, strong_left, strong_right, strong_energy, weak_amp, weak_rhs,
        weak_blocks, weak_energy, strong_intersection, weak_intersection,
    )
    amp1, tiles1, col_out1, *row_out1 = call(
        strong_kernel,
        [(s_shape, F32), (s_shape, BF16), col_shape] + row_shapes,
        [SM] * 6 + [HB, ANY] + [HB] * 4 + [ANY] * (nr - 1),
        s_flops // 2, s_bytes,
        [
            pool, s_all, s_sums, s_f32, s_f32, s_bf16, s_items, sem((pool_sems + sent_sems + 3,)),
            sem((sp,)),
        ],
    )(
        me, s_order, s_near, strong_live, col_send, row_send, tiles, got, strong_intersection,
        s_acc, s_inv, strong_amp, *row_got,
    )
    got1, row_got1 = exchange(col_out1, row_out1)
    w_amp1, s_acc1, w_acc1 = call(
        functools.partial(middle_kernel, nc),
        [(w_shape, F32), (s_shape, F32), (w_shape, F32)],
        [SM] * 8 + [HB, ANY] + [HB] * 11 + [ANY] * (nr - 1),
        a_flops + s_flops // 2 + w_flops, s_bytes + w_bytes,
        [
            pool, pool, w_sums, w_f32, w_f32, w_f32, blocks, s_f32, s_bf16, s_bf16, s_all, w_all,
            s_sums, s_items, w_items, sem((2 * pool_sems + 12,)), sem((2, max(sp, wp))),
        ],
    )(
        me, s_order, s_near, strong_live, w_order, w_near, col_send, row_send,
        tiles, got, tiles1, w_acc, w_inv, weak_amp, weak_rhs, weak_blocks, strong_rhs, strong_left,
        strong_right, strong_intersection, weak_intersection, *row_got,
    )
    s_out, w_out = call(
        last_kernel,
        [(s_shape, F32), (w_shape, F32)],
        [SM] * 7 + [HB, ANY] + [HB] * 8 + [ANY] * (nr - 1),
        (s_flops + w_flops) // 2, s_bytes + w_bytes,
        [
            pool, s_all, w_all, s_sums, w_sums, s_f32, w_f32, s_f32, w_f32, s_items, w_items,
            sem((pool_sems + 10,)), sem((sp,)), sem((wp,)),
        ],
    )(
        me, s_order, s_near, strong_live, w_order, w_near, row_send, tiles1, got1,
        strong_intersection, weak_intersection, s_acc1, w_acc1, s_inv, w_inv, amp1, w_amp1,
        *row_got1,
    )
    return s_out, w_out


def solution(mesh):
    nr, nc = mesh.shape["row"], mesh.shape["col"]
    whole = ("row", "col")
    ranks = (3, 3, 3, 3, 2, 4, 2, 1, 2, 2, 3, 3, 3, 2, 4, 2)
    in_specs = tuple(P(whole, *(None,) * (r - 1)) for r in ranks)
    out_specs = (P(whole, None, None), P(whole, None, None))
    return jax.shard_map(
        functools.partial(on_device, nr, nc),
        mesh=mesh, in_specs=in_specs, out_specs=out_specs, check_vma=False,
    )
```

```python
import functools

import jax
import jax.numpy as jnp
from jax import lax
from jax.experimental import pallas as pl
from jax.experimental.pallas import tpu as pltpu
from jax.sharding import PartitionSpec as P

F32 = jnp.float32
BF16 = jnp.bfloat16
MIB = 1 << 20
GROUP = 4
STRONG_ITEMS = 4


VM = pl.BlockSpec(memory_space=pltpu.VMEM)
SM = pl.BlockSpec(memory_space=pltpu.SMEM)
HB = pl.BlockSpec(memory_space=pltpu.HBM)
ANY = pl.BlockSpec(memory_space=pl.ANY)


def call(body, outs, in_specs, flops, nbytes, scratch):
    return pl.pallas_call(
        body,
        out_shape=[jax.ShapeDtypeStruct(s, d) for s, d in outs],
        in_specs=in_specs,
        out_specs=[HB for _ in outs],
        scratch_shapes=list(scratch),
        cost_estimate=pl.CostEstimate(
            flops=int(flops), bytes_accessed=int(nbytes), transcendentals=0
        ),
        compiler_params=pltpu.CompilerParams(vmem_limit_bytes=58 * MIB),
    )


class Copies:
    def __init__(self, sems):
        self.sems, self.used, self.named = sems, 0, {}

    def start(self, name, src, dst):
        copy = pltpu.make_async_copy(src, dst, self.sems.at[self.used])
        self.used += 1
        self.named.setdefault(name, []).append(copy)
        copy.start()

    def wait(self, *names):
        for name in names:
            for copy in self.named.pop(name):
                copy.wait()


def dot(a, b):
    return jnp.dot(a, b, preferred_element_type=F32)


def dot_t(a, b):
    return lax.dot_general(a, b, (((1,), (1,)), ((), ())), preferred_element_type=F32)


def partner(i, k, n):
    return i ^ k if n & (n - 1) == 0 else lax.rem(i + k, n)


def origin(i, k, n):
    return i ^ k if n & (n - 1) == 0 else lax.rem(i + n - k, n)


def perm(k, n):
    if n & (n - 1) == 0:
        return [(s, s ^ k) for s in range(n)]
    return [(s, (s + k) % n) for s in range(n)]


def each(n, f, unroll=1):
    if n % unroll:
        unroll = 1

    def body(i, c):
        for u in range(unroll):
            f(i * unroll + u)
        return c

    lax.fori_loop(0, n // unroll, body, 0)


def position():
    return lax.axis_index("row"), lax.axis_index("col")


def start_sends(copies, me, tiles, col_send, row_send, col_out, row_out):
    cap = col_out.shape[1]
    for d in range(col_out.shape[0]):
        for s in range(cap):
            copies.start("sent", tiles.at[col_send[s, d]], col_out.at[d, s])
    n = len(row_out) + 1
    for k in range(1, n):
        d = partner(me[0], k, n)
        for s in range(cap):
            copies.start("sent", tiles.at[row_send[s, d]], row_out[k - 1].at[s])


def prep_kernel(col_send_h, row_send_h, amp_h, tiles_out, col_out, *rest):
    *row_out, amp, tiles, col_send, row_send, sems = rest
    me = position()
    copies = Copies(sems)
    parts = 4
    step = amp.shape[0] // parts
    copies.start("lists", col_send_h, col_send)
    copies.start("lists", row_send_h, row_send)
    for i in range(parts):
        at = pl.ds(i * step, step)
        copies.start(i, amp_h.at[at], amp.at[at])
    for i in range(parts):
        copies.wait(i)
        for j in range(step):
            tiles[i * step + j] = amp[i * step + j].astype(BF16)
    copies.wait("lists")
    start_sends(copies, me, tiles, col_send, row_send, col_out, row_out)
    copies.start("sent", tiles, tiles_out)
    copies.wait("sent")


def weak_inter(blocks, t):
    q = t.shape[0]
    return dot(blocks[:, :q], t) + dot(t, blocks[:, q:])


def strong_inter(left, right, t):
    return dot(left, t) + dot(t, right)


def inverse(e):
    n = e.shape[1]
    rows = jnp.broadcast_to(e, (n, n))
    return 1.0 / (rows.T + rows)


def start_near(copies, me, tiles, col_send, row_send, pool, nc):
    own = tiles.shape[0]
    cap = col_send.shape[0]
    copies.start("near", tiles, pool.at[pl.ds(0, own)])
    for s in range(cap):
        copies.start("near", tiles.at[col_send[s, me[1]]], pool.at[own + me[1] * cap + s])
        copies.start(
            "near", tiles.at[row_send[s, me[0]]], pool.at[own + (nc + me[0]) * cap + s]
        )


def start_pool(copies, me, tiles, row_send, pool, got, row_got):
    own = tiles.shape[0]
    nc, cap = got.shape[:2]
    copies.start("near", tiles, pool.at[pl.ds(0, own)])
    for c in range(nc):
        copies.start("near", got.at[c], pool.at[pl.ds(own + c * cap, cap)])
    at = own + nc * cap
    n = len(row_got) + 1
    for s in range(cap):
        copies.start("near", tiles.at[row_send[s, me[0]]], pool.at[at + me[0] * cap + s])
    for k in range(1, n):
        o = origin(me[0], k, n)
        copies.start("near", row_got[k - 1], pool.at[pl.ds(at + o * cap, cap)])


class Rows:
    def __init__(self, src, dst, sems):
        self.src, self.dst, self.sems = src, dst, sems
        self.n = dst.shape[0]

    def copy(self, i):
        return pltpu.make_async_copy(self.src.at[i], self.dst.at[i], self.sems.at[i])

    def start(self):
        for i in range(self.n):
            self.copy(i).start()

    def wait_one(self, i):
        self.copy(i).wait()

    def wait(self, ready, upto):
        def one(i, c):
            self.copy(i).wait()
            return c

        lax.fori_loop(ready, upto, one, 0)
        return jnp.maximum(ready, upto)


def live_items(items, n, live, step):
    def one(p, at):
        for j in range(4):
            items[at + j] = p * 4 + j
        return at + ((live[p] + GROUP - 1) >> 2)

    count = lax.fori_loop(0, n, one, 0)
    for j in range(step):
        items[count + j] = n * 4
    return (count + step - 1) // step


def clear(mids):
    zero = jnp.zeros(mids.shape[1:], mids.dtype)
    each(mids.shape[0], lambda p: mids.__setitem__(p, zero))


def strong_mids(steps, items, pool, nb, live, inter, rows, mids):
    n = inter.shape[0]

    def body(i, ready):
        last = jnp.minimum(items[i * STRONG_ITEMS + STRONG_ITEMS - 1] >> 2, n - 1)
        ready = rows.wait(ready, last + 1)
        for u in range(STRONG_ITEMS):
            item = items[i * STRONG_ITEMS + u]
            at = item >> 2
            p = jnp.minimum(at, n - 1)
            for g in range(GROUP):
                k = (item & 3) * GROUP + g
                m = dot(inter[p, k], pool[nb[p, k]]).astype(BF16)
                mids[at, k] = jnp.where(k < live[p], m, jnp.zeros_like(m))
        return ready

    ready = lax.fori_loop(0, steps, body, jnp.int32(0))
    rows.wait(ready, n)


def weak_mids(pool, nb, inter, rows, mids):
    def one(w):
        rows.wait_one(w)
        for k in range(inter.shape[1]):
            mids[w, k] = dot(inter[w, k], pool[nb[w, k]]).astype(BF16)

    def body(i, c):
        for u in range(4):
            rows.wait_one(i * 4 + u)
        for u in range(4):
            w = i * 4 + u
            for k in range(inter.shape[1]):
                mids[w, k] = dot(inter[w, k], pool[nb[w, k]]).astype(BF16)
        return c

    n = inter.shape[0]
    if n % 4:
        each(n, one)
    else:
        lax.fori_loop(0, n // 4, body, 0)


def folded(p, mids, inter):
    count = inter.shape[1]
    return dot_t(
        jnp.concatenate([mids[p, k] for k in range(count)], axis=1),
        jnp.concatenate([inter[p, k] for k in range(count)], axis=1),
    )


def first_kernel(
    tiles_h, s_rhs_h, s_left_h, s_right_h, s_energy_h, w_amp_h, w_rhs_h, w_blocks_h, w_energy_h,
    s_base_out, w_base_out, s_inv_out, w_inv_out,
    tiles, s_rhs, s_left, s_right, s_energy, w_amp, w_rhs, w_blocks, w_energy, s_inv, w_inv, sems,
):
    copies = Copies(sems)
    for src, dst in (
        (tiles_h, tiles), (s_left_h, s_left), (s_right_h, s_right), (s_rhs_h, s_rhs),
        (s_energy_h, s_energy),
    ):
        copies.start("s", src, dst)
    for src, dst in ((w_amp_h, w_amp), (w_blocks_h, w_blocks), (w_rhs_h, w_rhs), (w_energy_h, w_energy)):
        copies.start("w", src, dst)
    copies.wait("s")

    def strong(p):
        s_rhs[p] += strong_inter(s_left[p], s_right[p], tiles[p])
        s_inv[p] = inverse(s_energy[pl.ds(p, 1), :])

    each(s_rhs.shape[0], strong, 2)
    copies.start("out", s_inv, s_inv_out)
    copies.start("out", s_rhs, s_base_out)
    copies.wait("w")

    def weak(w):
        w_rhs[w] += weak_inter(w_blocks[w], w_amp[w].astype(BF16))
        w_inv[w] = inverse(w_energy[pl.ds(w, 1), :])

    each(w_amp.shape[0], weak, 4)
    copies.start("out", w_inv, w_inv_out)
    copies.start("out", w_rhs, w_base_out)
    copies.wait("out")


def strong_kernel(
    nb, live, col_send, row_send, tiles_h, got, s_int_h, s_base_h, s_inv_h, amp_h, *rest,
):
    n_row = (len(rest) - 13) // 2
    row_got, (amp_out, tiles_out, col_out), row_out = (
        rest[:n_row], rest[n_row : n_row + 3], rest[n_row + 3 : 2 * n_row + 3]
    )
    pool, s_all, mids, s_base, s_inv, amp, tiles, items, sems, s_sems = rest[2 * n_row + 3 :]
    n = amp.shape[0]
    me = position()
    copies = Copies(sems)
    start_pool(copies, me, tiles_h, row_send, pool, got, row_got)
    rows = Rows(s_int_h, s_all, s_sems)
    rows.start()
    for src, dst in ((amp_h, amp), (s_base_h, s_base), (s_inv_h, s_inv)):
        copies.start("end", src, dst)
    clear(mids)
    steps = live_items(items, n, live, STRONG_ITEMS)
    copies.wait("near")
    strong_mids(steps, items, pool, nb, live, s_all, rows, mids)
    copies.wait("end")

    def finish(p):
        new = amp[p] - (s_base[p] + folded(p, mids, s_all)) * s_inv[p]
        amp[p] = new
        tiles[p] = new.astype(BF16)

    each(n, finish, 4)
    start_sends(copies, me, tiles, col_send, row_send, col_out, row_out)
    copies.start("sent", tiles, tiles_out)
    copies.start("sent", amp, amp_out)
    copies.wait("sent")


def middle_kernel(
    w_nb, row_send, tiles_h, got, tiles1_h, w_base_h, w_inv_h, w_amp_h, w_rhs_h, w_blocks_h,
    s_rhs_h, s_left_h, s_right_h, w_int_h, *rest,
):
    n_row = len(rest) - 17
    row_got, (w_out, w_base_out, s_base_out) = rest[:n_row], rest[n_row : n_row + 3]
    (
        pool, w_all, mids, w_base, w_inv, w_amp, w_rhs, w_blocks, tiles, s_rhs, s_left, s_right,
        sems, w_sems,
    ) = rest[n_row + 3 :]
    copies = Copies(sems)
    start_pool(copies, position(), tiles_h, row_send, pool, got, row_got)
    rows = Rows(w_int_h, w_all, w_sems)
    rows.start()
    for src, dst in (
        (w_base_h, w_base), (w_inv_h, w_inv), (w_amp_h, w_amp), (w_rhs_h, w_rhs),
        (w_blocks_h, w_blocks),
    ):
        copies.start("w", src, dst)
    for src, dst in ((tiles1_h, tiles), (s_left_h, s_left), (s_right_h, s_right), (s_rhs_h, s_rhs)):
        copies.start("s", src, dst)
    copies.wait("near")
    weak_mids(pool, w_nb, w_all, rows, mids)
    copies.wait("w")

    def weak(w):
        w_amp[w] = w_amp[w] - (w_base[w] + folded(w, mids, w_all)) * w_inv[w]

    each(w_amp.shape[0], weak, 4)
    copies.start("out", w_amp, w_out)

    def base(w):
        w_rhs[w] += weak_inter(w_blocks[w], w_amp[w].astype(BF16))

    each(w_amp.shape[0], base, 4)
    copies.start("out", w_rhs, w_base_out)
    copies.wait("s")

    def strong(p):
        s_rhs[p] += strong_inter(s_left[p], s_right[p], tiles[p])

    each(s_rhs.shape[0], strong, 2)
    copies.start("out", s_rhs, s_base_out)
    copies.wait("out")


def last_kernel(
    s_nb, live, w_nb, row_send, tiles_h, got, s_int_h, w_int_h, s_base_h, w_base_h, s_inv_h,
    w_inv_h, s_amp_h, w_amp_h, *rest,
):
    n_row = len(rest) - 17
    row_got, (s_out, w_out) = rest[:n_row], rest[n_row : n_row + 2]
    (
        pool, s_all, w_all, s_mids, w_mids, s_base, w_base, s_inv, w_inv, s_amp, w_amp, items, sems,
        s_sems, w_sems,
    ) = rest[n_row + 2 :]
    n, wp = s_amp.shape[0], w_amp.shape[0]
    copies = Copies(sems)
    start_pool(copies, position(), tiles_h, row_send, pool, got, row_got)
    s_rows, w_rows = Rows(s_int_h, s_all, s_sems), Rows(w_int_h, w_all, w_sems)
    s_rows.start()
    for src, dst in ((s_amp_h, s_amp), (s_base_h, s_base), (s_inv_h, s_inv)):
        copies.start("s", src, dst)
    w_rows.start()
    for src, dst in ((w_amp_h, w_amp), (w_base_h, w_base), (w_inv_h, w_inv)):
        copies.start("w", src, dst)
    clear(s_mids)
    steps = live_items(items, n, live, STRONG_ITEMS)
    copies.wait("near")
    strong_mids(steps, items, pool, s_nb, live, s_all, s_rows, s_mids)
    copies.wait("s")

    def strong(p):
        s_amp[p] = s_amp[p] - (s_base[p] + folded(p, s_mids, s_all)) * s_inv[p]

    each(n, strong, 4)
    copies.start("out", s_amp, s_out)
    weak_mids(pool, w_nb, w_all, w_rows, w_mids)
    copies.wait("w")

    def weak(w):
        w_amp[w] = w_amp[w] - (w_base[w] + folded(w, w_mids, w_all)) * w_inv[w]

    each(wp, weak, 4)
    copies.start("out", w_amp, w_out)
    copies.wait("out")


def on_device(
    nr, nc, strong_amp, strong_rhs, strong_left, strong_right, strong_energy, strong_intersection,
    strong_nb, strong_live, col_send, row_send, weak_amp, weak_rhs, weak_blocks, weak_energy,
    weak_intersection, weak_nb,
):
    sp, width = strong_amp.shape[:2]
    wp, q = weak_amp.shape[:2]
    count = strong_nb.shape[1]
    cap = col_send.shape[1]
    col_lists, row_lists = col_send.T, row_send.T
    s_shape, w_shape = (sp, width, width), (wp, q, q)
    s_f32, w_f32 = pltpu.VMEM(s_shape, F32), pltpu.VMEM(w_shape, F32)
    s_bf16, blocks = pltpu.VMEM(s_shape, BF16), pltpu.VMEM(weak_blocks.shape, BF16)
    s_all = pltpu.VMEM(strong_intersection.shape, BF16)
    w_all = pltpu.VMEM(weak_intersection.shape, BF16)
    s_mids = pltpu.VMEM((sp + 1, count, width, width), BF16)
    w_mids = pltpu.VMEM((wp, count, q, width), BF16)
    pool = pltpu.VMEM((sp + cap * (nc + nr), width, width), BF16)
    row_shapes = [((cap, width, width), BF16)] * (nr - 1)
    col_shape = ((nc, cap, width, width), BF16)
    s_flops = 4 * sp * count * width**3
    w_flops = 2 * wp * count * (q * width * width + q * q * width)
    a_flops = 4 * sp * width**3
    s_bytes, w_bytes = strong_intersection.size * 2, weak_intersection.size * 2
    s_items = pltpu.SMEM((sp * count // GROUP + GROUP + STRONG_ITEMS,), jnp.int32)
    sem = pltpu.SemaphoreType.DMA
    pool_sems = nc + nr + cap + 4 * cap
    sent_sems = cap * (nc + nr) + 2

    def exchange(col_out, row_out):
        got = lax.all_to_all(col_out, "col", split_axis=0, concat_axis=0, tiled=True)
        return got, [lax.ppermute(x, "row", perm(k + 1, nr)) for k, x in enumerate(row_out)]

    tiles, col_out, *row_out = call(
        prep_kernel,
        [(s_shape, BF16), col_shape] + row_shapes,
        [HB, HB, HB],
        0, strong_amp.size * 8,
        [
            s_f32, s_bf16, pltpu.SMEM(col_lists.shape, jnp.int32),
            pltpu.SMEM(row_lists.shape, jnp.int32), sem((sent_sems + 6,)),
        ],
    )(col_lists, row_lists, strong_amp)
    got, row_got = exchange(col_out, row_out)
    s_base, w_base, s_inv, w_inv = call(
        first_kernel,
        [(s_shape, F32), (w_shape, F32)] * 2,
        [HB] * 9,
        a_flops, strong_amp.size * 24,
        [
            s_bf16, s_f32, s_bf16, s_bf16, pltpu.VMEM(strong_energy.shape, F32), w_f32, w_f32,
            blocks, pltpu.VMEM(weak_energy.shape, F32), s_f32, w_f32, sem((13,)),
        ],
    )(
        tiles, strong_rhs, strong_left, strong_right, strong_energy, weak_amp, weak_rhs,
        weak_blocks, weak_energy,
    )
    amp1, tiles1, col_out1, *row_out1 = call(
        strong_kernel,
        [(s_shape, F32), (s_shape, BF16), col_shape] + row_shapes,
        [SM] * 4 + [HB, ANY] + [HB] * 4 + [ANY] * (nr - 1),
        s_flops, s_bytes,
        [
            pool, s_all, s_mids, s_f32, s_f32, s_f32, s_bf16, s_items,
            sem((pool_sems + sent_sems + 3,)), sem((sp,)),
        ],
    )(
        strong_nb, strong_live, col_lists, row_lists, tiles, got, strong_intersection, s_base,
        s_inv, strong_amp, *row_got,
    )
    got1, row_got1 = exchange(col_out1, row_out1)
    w_amp1, w_base1, s_base1 = call(
        middle_kernel,
        [(w_shape, F32), (w_shape, F32), (s_shape, F32)],
        [SM] * 2 + [HB, ANY] + [HB] * 10 + [ANY] * (nr - 1),
        a_flops + w_flops, w_bytes,
        [
            pool, w_all, w_mids, w_f32, w_f32, w_f32, w_f32, blocks, s_bf16, s_f32, s_bf16, s_bf16,
            sem((pool_sems + 12,)), sem((wp,)),
        ],
    )(
        weak_nb, row_lists, tiles, got, tiles1, w_base, w_inv, weak_amp, weak_rhs, weak_blocks,
        strong_rhs, strong_left, strong_right, weak_intersection, *row_got,
    )
    s_out, w_out = call(
        last_kernel,
        [(s_shape, F32), (w_shape, F32)],
        [SM] * 4 + [HB, ANY] + [HB] * 8 + [ANY] * (nr - 1),
        s_flops + w_flops, s_bytes + w_bytes,
        [
            pool, s_all, w_all, s_mids, w_mids, s_f32, w_f32, s_f32, w_f32, s_f32, w_f32, s_items,
            sem((pool_sems + 8,)), sem((sp,)), sem((wp,)),
        ],
    )(
        strong_nb, strong_live, weak_nb, row_lists, tiles1, got1, strong_intersection,
        weak_intersection, s_base1, w_base1, s_inv, w_inv, amp1, w_amp1, *row_got1,
    )
    return s_out, w_out


def solution(mesh):
    nr, nc = mesh.shape["row"], mesh.shape["col"]
    whole = ("row", "col")
    ranks = (3, 3, 3, 3, 2, 4, 2, 1, 2, 2, 3, 3, 3, 2, 4, 2)
    in_specs = tuple(P(whole, *(None,) * (r - 1)) for r in ranks)
    out_specs = (P(whole, None, None), P(whole, None, None))
    return jax.shard_map(
        functools.partial(on_device, nr, nc),
        mesh=mesh, in_specs=in_specs, out_specs=out_specs, check_vma=False,
    )
```

```python
import functools

import jax
import jax.numpy as jnp
from jax import lax
from jax.experimental import pallas as pl
from jax.experimental.pallas import tpu as pltpu
from jax.sharding import PartitionSpec as P

F32 = jnp.float32
BF16 = jnp.bfloat16
MIB = 1 << 20


VM = pl.BlockSpec(memory_space=pltpu.VMEM)
SM = pl.BlockSpec(memory_space=pltpu.SMEM)
HB = pl.BlockSpec(memory_space=pltpu.HBM)
ANY = pl.BlockSpec(memory_space=pl.ANY)


def call(body, outs, in_specs, flops, nbytes, scratch, limit=58, out_specs=None):
    run = pl.pallas_call(
        body,
        out_shape=[jax.ShapeDtypeStruct(s, d) for s, d in outs],
        in_specs=in_specs,
        out_specs=out_specs or [HB for _ in outs],
        scratch_shapes=list(scratch),
        cost_estimate=pl.CostEstimate(
            flops=int(flops), bytes_accessed=int(nbytes), transcendentals=0
        ),
        compiler_params=pltpu.CompilerParams(vmem_limit_bytes=limit * MIB),
    )

    def pinned(*args):
        return run(
            *(
                pltpu.with_memory_space_constraint(a, pltpu.HBM) if spec is HB else a
                for a, spec in zip(args, in_specs, strict=True)
            )
        )

    return pinned


class Copies:
    def __init__(self, sems):
        self.sems, self.used, self.named = sems, 0, {}

    def start(self, name, src, dst):
        copy = pltpu.make_async_copy(src, dst, self.sems.at[self.used])
        self.used += 1
        self.named.setdefault(name, []).append(copy)
        copy.start()

    def wait(self, *names):
        for name in names:
            for copy in self.named.pop(name):
                copy.wait()


def dot(a, b):
    return jnp.dot(a, b, preferred_element_type=F32)


def dot_t(a, b):
    return lax.dot_general(a, b, (((1,), (1,)), ((), ())), preferred_element_type=F32)


def partner(i, k, n):
    return i ^ k if n & (n - 1) == 0 else lax.rem(i + k, n)


def origin(i, k, n):
    return i ^ k if n & (n - 1) == 0 else lax.rem(i + n - k, n)


def perm(k, n):
    if n & (n - 1) == 0:
        return [(s, s ^ k) for s in range(n)]
    return [(s, (s + k) % n) for s in range(n)]


def each(n, f, unroll=1):
    if n % unroll:
        unroll = 1

    def body(i, c):
        for u in range(unroll):
            f(i * unroll + u)
        return c

    lax.fori_loop(0, n // unroll, body, 0)


def position():
    return lax.axis_index("row"), lax.axis_index("col")


def start_sends(copies, me, tiles, col_send, row_send, col_out, row_out):
    cap = col_out.shape[1]
    for d in range(col_out.shape[0]):
        for s in range(cap):
            copies.start("sent", tiles.at[col_send[s, d]], col_out.at[d, s])
    n = len(row_out) + 1
    for k in range(1, n):
        d = partner(me[0], k, n)
        for s in range(cap):
            copies.start("sent", tiles.at[row_send[s, d]], row_out[k - 1].at[s])


def prep_kernel(col_send_h, row_send_h, amp_h, tiles_out, col_out, *rest):
    *row_out, amp, tiles, col_send, row_send, sems = rest
    me = position()
    copies = Copies(sems)
    parts = 4
    step = amp.shape[0] // parts
    copies.start("lists", col_send_h, col_send)
    copies.start("lists", row_send_h, row_send)
    for i in range(parts):
        at = pl.ds(i * step, step)
        copies.start(i, amp_h.at[at], amp.at[at])
    for i in range(parts):
        copies.wait(i)
        for j in range(step):
            tiles[i * step + j] = amp[i * step + j].astype(BF16)
    copies.wait("lists")
    start_sends(copies, me, tiles, col_send, row_send, col_out, row_out)
    copies.start("sent", tiles, tiles_out)
    copies.wait("sent")


def weak_inter(blocks, t):
    q = t.shape[0]
    return dot(blocks[:, :q], t) + dot(t, blocks[:, q:])


def strong_inter(left, right, t):
    return dot(left, t) + dot(t, right)


def inverse(e):
    n = e.shape[1]
    rows = jnp.broadcast_to(e, (n, n))
    return 1.0 / (rows.T + rows)


def start_pool(copies, me, tiles, row_send, pool, got, row_got):
    own = tiles.shape[0]
    nc, cap = got.shape[:2]
    copies.start("near", tiles, pool.at[pl.ds(0, own)])
    for c in range(nc):
        copies.start("near", got.at[c], pool.at[pl.ds(own + c * cap, cap)])
    at = own + nc * cap
    n = len(row_got) + 1
    for s in range(cap):
        copies.start("near", tiles.at[row_send[s, me[0]]], pool.at[at + me[0] * cap + s])
    for k in range(1, n):
        o = origin(me[0], k, n)
        copies.start("near", row_got[k - 1], pool.at[pl.ds(at + o * cap, cap)])


class Rows:
    def __init__(self, src, dst, sems):
        self.src, self.dst, self.sems = src, dst, sems
        self.n = dst.shape[0]

    def copy(self, i):
        return pltpu.make_async_copy(self.src.at[i], self.dst.at[i], self.sems.at[i])

    def start(self, first, past):
        for i in range(first, past):
            self.copy(i).start()

    def wait(self, first, past):
        for i in range(first, past):
            self.copy(i).wait()


def pair_mids(p, pool, nb, live, inter, mids):
    for k in range(inter.shape[1]):
        m = dot(inter[p, k], pool[nb[p, k]]).astype(BF16)
        if live is not None:
            m = jnp.where(k < live[p], m, jnp.zeros_like(m))
        mids[p, k] = m


def all_mids(pool, nb, live, inter, rows, mids, then=None):
    n = inter.shape[0]
    parts = max(n // 8, 1)
    for i in range(parts):
        first, past = n * i // parts, n * (i + 1) // parts
        if rows is not None:
            rows.wait(first, past)
        if then is not None:
            then(i)
        for p in range(first, past):
            pair_mids(p, pool, nb, live, inter, mids)


def folded(p, mids, inter):
    count = inter.shape[1]
    return dot_t(
        jnp.concatenate([mids[p, k] for k in range(count)], axis=1),
        jnp.concatenate([inter[p, k] for k in range(count)], axis=1),
    )


def fill_inverse(inv, energy, unroll):
    each(inv.shape[0], lambda p: inv.__setitem__(p, inverse(energy[pl.ds(p, 1), :])), unroll)


def first_kernel(
    tiles_h, s_amp_h, s_rhs_h, s_left_h, s_right_h, s_energy_h, w_amp_h, w_rhs_h, w_blocks_h,
    w_energy_h,
    s_rest_out, w_rest_out,
    tiles, s_amp, s_rhs, s_left, s_right, s_energy, w_amp, w_rhs, w_blocks, w_energy, sems,
):
    copies = Copies(sems)
    for src, dst in (
        (tiles_h, tiles), (s_left_h, s_left), (s_right_h, s_right), (s_rhs_h, s_rhs),
        (s_energy_h, s_energy), (s_amp_h, s_amp),
    ):
        copies.start("s", src, dst)
    for src, dst in ((w_amp_h, w_amp), (w_blocks_h, w_blocks), (w_rhs_h, w_rhs), (w_energy_h, w_energy)):
        copies.start("w", src, dst)
    copies.wait("s")

    def strong(p):
        base = s_rhs[p] + strong_inter(s_left[p], s_right[p], tiles[p])
        s_amp[p] -= base * inverse(s_energy[pl.ds(p, 1), :])

    each(s_rhs.shape[0], strong, 4)
    copies.start("out", s_amp, s_rest_out)
    copies.wait("w")

    def weak(w):
        amp = w_amp[w]
        base = w_rhs[w] + weak_inter(w_blocks[w], amp.astype(BF16))
        w_amp[w] = amp - base * inverse(w_energy[pl.ds(w, 1), :])

    each(w_amp.shape[0], weak, 4)
    copies.start("out", w_amp, w_rest_out)
    copies.wait("out")


def strong_kernel(
    nb, live, col_send, row_send, tiles_h, got, s_int_h, w_int_h, s_rest_h, s_energy_h, *rest,
):
    n_row = row_send.shape[1] - 1
    n_sent = n_row + col_send.shape[1] - 1
    row_got, (s_all, w_all, pool, amp, tiles, s_inv) = rest[:n_row], rest[n_row : n_row + 6]
    sends = rest[n_row + 6 : n_row + 6 + n_sent]
    mids, s_rest, s_energy, sems, s_sems, w_sems = rest[n_row + 6 + n_sent :]
    n, wp = amp.shape[0], w_all.shape[0]
    me = position()
    copies = Copies(sems)
    copies.start("energy", s_energy_h, s_energy)
    start_pool(copies, me, tiles_h, row_send, pool, got, row_got)
    rows, w_rows = Rows(s_int_h, s_all, s_sems), Rows(w_int_h, w_all, w_sems)
    rows.start(0, n // 2)
    copies.wait("energy")
    fill_inverse(s_inv, s_energy, 4)
    rows.start(n // 2, n)
    copies.start("end", s_rest_h, s_rest)
    copies.wait("near")

    def then(i):
        if i == max(n // 8, 1) - 1:
            w_rows.start(0, wp)

    all_mids(pool, nb, live, s_all, rows, mids, then)
    copies.wait("end")

    def finish(p):
        new = s_rest[p] - folded(p, mids, s_all) * s_inv[p]
        amp[p] = new
        tiles[p] = new.astype(BF16)

    each(n, finish, 8)
    at = 0
    for lists, i in ((col_send, me[1]), (row_send, me[0])):
        for k in range(1, lists.shape[1]):
            d = partner(i, k, lists.shape[1])
            for c in range(lists.shape[0]):
                sends[at][c] = tiles[lists[c, d]]
            at += 1
    w_rows.wait(0, wp)


def middle_kernel(
    w_nb, pool, w_all, tiles, s_amp, s_inv, w_rest_h, w_energy_h, w_rhs_h, w_blocks_h, s_rhs_h,
    s_left_h, s_right_h,
    w_amp, s_rest, w_inv, mids, w_energy, w_rhs, w_blocks, s_rhs, s_left, s_right, sems,
):
    wp = w_amp.shape[0]
    copies = Copies(sems)
    copies.start("energy", w_energy_h, w_energy)
    for src, dst in ((s_left_h, s_left), (s_right_h, s_right), (s_rhs_h, s_rhs)):
        copies.start("s", src, dst)
    for src, dst in ((w_rest_h, w_amp), (w_rhs_h, w_rhs), (w_blocks_h, w_blocks)):
        copies.start("w", src, dst)
    all_mids(pool, w_nb, None, w_all, None, mids)
    copies.wait("energy")
    fill_inverse(w_inv, w_energy, 8)
    copies.wait("w")

    def weak(w):
        w_amp[w] -= folded(w, mids, w_all) * w_inv[w]

    each(wp, weak, 8)

    def base(w):
        amp = w_amp[w]
        w_amp[w] = amp - (w_rhs[w] + weak_inter(w_blocks[w], amp.astype(BF16))) * w_inv[w]

    each(wp, base, 8)
    copies.wait("s")

    def strong(p):
        base = s_rhs[p] + strong_inter(s_left[p], s_right[p], tiles[p])
        s_rest[p] = s_amp[p] - base * s_inv[p]

    each(s_rhs.shape[0], strong, 4)


def last_kernel(
    s_nb, live, w_nb, col_send, row_send, tiles, s_all, w_all, s_rest, w_rest, s_inv, w_inv, *rest,
):
    nc, nr = col_send.shape[1], row_send.shape[1]
    got, (s_out, w_out) = rest[: nc + nr - 2], rest[nc + nr - 2 : nc + nr]
    pool, s_mids, w_mids, s_new, w_new, sems = rest[nc + nr :]
    n, wp = tiles.shape[0], w_rest.shape[0]
    cap = col_send.shape[0]
    me = position()
    copies = Copies(sems)
    for p in range(n):
        pool[p] = tiles[p]
    at, first = n, 0
    for lists, i in ((col_send, me[1]), (row_send, me[0])):
        many = lists.shape[1]
        for c in range(cap):
            pool[at + i * cap + c] = tiles[lists[c, i]]
        for k in range(1, many):
            for c in range(cap):
                pool[at + origin(i, k, many) * cap + c] = got[first + k - 1][c]
        at += many * cap
        first += many - 1
    all_mids(pool, s_nb, live, s_all, None, s_mids)

    def strong(p):
        s_new[p] = s_rest[p] - folded(p, s_mids, s_all) * s_inv[p]

    each(n, strong, 8)
    copies.start("out", s_new, s_out)
    all_mids(pool, w_nb, None, w_all, None, w_mids)

    def weak(w):
        w_new[w] = w_rest[w] - folded(w, w_mids, w_all) * w_inv[w]

    each(wp, weak, 8)
    copies.start("out", w_new, w_out)
    copies.wait("out")


def on_device(
    nr, nc, strong_amp, strong_rhs, strong_left, strong_right, strong_energy, strong_intersection,
    strong_nb, strong_live, col_send, row_send, weak_amp, weak_rhs, weak_blocks, weak_energy,
    weak_intersection, weak_nb,
):
    sp, width = strong_amp.shape[:2]
    wp, q = weak_amp.shape[:2]
    count = strong_nb.shape[1]
    cap = col_send.shape[1]
    col_lists, row_lists = col_send.T, row_send.T
    s_shape, w_shape = (sp, width, width), (wp, q, q)
    s_f32, w_f32 = pltpu.VMEM(s_shape, F32), pltpu.VMEM(w_shape, F32)
    s_bf16, blocks = pltpu.VMEM(s_shape, BF16), pltpu.VMEM(weak_blocks.shape, BF16)
    s_all = pltpu.VMEM(strong_intersection.shape, BF16)
    w_all = pltpu.VMEM(weak_intersection.shape, BF16)
    s_mids = pltpu.VMEM(strong_intersection.shape, BF16)
    w_mids = pltpu.VMEM(weak_intersection.shape, BF16)
    pool = pltpu.VMEM((sp + cap * (nc + nr), width, width), BF16)
    row_shapes = [((cap, width, width), BF16)] * (nr - 1)
    col_shape = ((nc, cap, width, width), BF16)
    s_flops = 4 * sp * count * width**3
    w_flops = 2 * wp * count * (q * width * width + q * q * width)
    a_flops = 4 * sp * width**3
    s_bytes, w_bytes = strong_intersection.size * 2, weak_intersection.size * 2
    sem = pltpu.SemaphoreType.DMA
    pool_sems = nc + nr + cap + 4 * cap
    sent_sems = cap * (nc + nr) + 2

    def exchange(col_out, row_out):
        got = lax.all_to_all(col_out, "col", split_axis=0, concat_axis=0, tiled=True)
        return got, [lax.ppermute(x, "row", perm(k + 1, nr)) for k, x in enumerate(row_out)]

    tiles, col_out, *row_out = call(
        prep_kernel,
        [(s_shape, BF16), col_shape] + row_shapes,
        [HB, HB, HB],
        0, strong_amp.size * 8,
        [
            s_f32, s_bf16, pltpu.SMEM(col_lists.shape, jnp.int32),
            pltpu.SMEM(row_lists.shape, jnp.int32), sem((sent_sems + 6,)),
        ],
    )(col_lists, row_lists, strong_amp)
    got, row_got = exchange(col_out, row_out)
    s_energy = pltpu.VMEM(strong_energy.shape, F32)
    w_energy = pltpu.VMEM(weak_energy.shape, F32)
    s_rest, w_rest = call(
        first_kernel,
        [(s_shape, F32), (w_shape, F32)],
        [HB] * 10,
        a_flops, strong_amp.size * 24,
        [s_bf16, s_f32, s_f32, s_bf16, s_bf16, s_energy, w_f32, w_f32, blocks, w_energy, sem((12,))],
    )(
        tiles, strong_amp, strong_rhs, strong_left, strong_right, strong_energy, weak_amp, weak_rhs,
        weak_blocks, weak_energy,
    )
    s_all, w_all, full_pool, amp1, tiles1, s_inv, *sends1 = call(
        strong_kernel,
        [
            (strong_intersection.shape, BF16), (weak_intersection.shape, BF16),
            (pool.shape, BF16), (s_shape, F32), (s_shape, BF16), (s_shape, F32),
        ] + [((cap, width, width), BF16)] * (nc + nr - 2),
        [SM] * 4 + [HB, ANY] + [HB] * 4 + [ANY] * (nr - 1),
        s_flops, s_bytes + w_bytes,
        [s_mids, s_f32, s_energy, sem((pool_sems + 3,)), sem((sp,)), sem((wp,))],
        12, [VM] * (6 + nc + nr - 2),
    )(
        strong_nb, strong_live, col_lists, row_lists, tiles, got, strong_intersection,
        weak_intersection, s_rest, strong_energy, *row_got,
    )
    far_first = sorted(range(1, nc), reverse=True)
    got1 = {k: lax.ppermute(sends1[k - 1], "col", perm(k, nc)) for k in far_first}
    got1 = [got1[k] for k in range(1, nc)]
    got1 += [lax.ppermute(sends1[nc - 2 + k], "row", perm(k, nr)) for k in range(1, nr)]
    w_rest1, s_rest1, w_inv = call(
        middle_kernel,
        [(w_shape, F32), (s_shape, F32), (w_shape, F32)],
        [SM] + [VM] * 5 + [HB] * 7,
        a_flops + w_flops, w_bytes,
        [w_mids, w_energy, w_f32, blocks, s_f32, s_bf16, s_bf16, sem((8,))],
        14, [VM] * 3,
    )(
        weak_nb, full_pool, w_all, tiles1, amp1, s_inv, w_rest, weak_energy, weak_rhs, weak_blocks,
        strong_rhs, strong_left, strong_right,
    )
    s_out, w_out = call(
        last_kernel,
        [(s_shape, F32), (w_shape, F32)],
        [SM] * 5 + [VM] * (7 + nc + nr - 2),
        s_flops + w_flops, s_bytes + w_bytes,
        [pool, s_mids, w_mids, s_f32, w_f32, sem((2,))],
        22,
    )(
        strong_nb, strong_live, weak_nb, col_lists, row_lists, tiles1, s_all, w_all, s_rest1,
        w_rest1, s_inv, w_inv, *got1,
    )
    return s_out, w_out


def solution(mesh):
    nr, nc = mesh.shape["row"], mesh.shape["col"]
    whole = ("row", "col")
    ranks = (3, 3, 3, 3, 2, 4, 2, 1, 2, 2, 3, 3, 3, 2, 4, 2)
    in_specs = tuple(P(whole, *(None,) * (r - 1)) for r in ranks)
    out_specs = (P(whole, None, None), P(whole, None, None))
    return jax.shard_map(
        functools.partial(on_device, nr, nc),
        mesh=mesh, in_specs=in_specs, out_specs=out_specs, check_vma=False,
    )
```
